512 devices in a mesh: gx: 32 (over x, y, core), gy: 16 (over z).
Axes of the slice: x: 4, y: 4, z: 16, core: 2. Of those that a mesh axis runs over, the one named last changes fastest.
Arguments:
- rhs: float32 [1024, 512, 128], P('gx', 'gy'), may hold values from -8 to 8, as said below
- heights: int32 [1024, 512], P('gx', 'gy'), may hold values from 0 to 63
- index_map: int32 [512], replicated, may hold values from 0 to 511, each once
- coarse_inverse: bfloat16 [512, 512], replicated, may hold values from 0 to 40, as said below
Outputs:
- solution: float32 [1024, 512, 128], P('gx', 'gy')
- residual: float32 [1024, 512, 128], P('gx', 'gy')
The draws below stay inside these ranges and needn't reach their ends.
Inputs may be any that keep to these rules, and one draw needn't show every extreme that they name: `rhs`: the rough part is at most 8 in size and the remaining part is small and positive. `coarse_inverse`: symmetric and positive definite.
All inputs are finite; a program needn't handle non-finite values.
Results may differ from the reference program's by a relative error of at most 0.0003.
Values sent between devices are 32-bit elements; how exact they have to be, the bound alone decides.
No kernel may reach another device: no remote copies, remote signals or barrier semaphores. Data moves between devices by JAX's collectives and lax.ppermute only.
A program may use at most 64 MiB of HBM per device.

```python
import jax
import jax.numpy as jnp
from jax import lax

CX = 32
CY = 32
NZ = 128
ITERS = 2
NX = 1024
NY = 512
NSUB = 512
N_GX = 32
N_GY = 16


def draw_rhs(key, part):
    rough_key = jax.random.fold_in(key, 11)
    coord_x = (jnp.arange(NX, dtype=jnp.float32) + 0.5) / NX
    coord_y = (jnp.arange(NY, dtype=jnp.float32) + 0.5) / NY
    rough = jnp.clip(jax.random.normal(rough_key, (NX, NY, NZ), jnp.float32), -5.0, 5.0)
    scale = 0.5 * jnp.exp(jnp.log(3.0) * coord_x)[:, None, None]
    smooth = 0.02 * (1.0 + 0.5 * jnp.cos(2.0 * jnp.pi * coord_x)[:, None, None] * jnp.sin(jnp.pi * coord_y)[None, :, None])
    return rough * scale + smooth


def draw_coarse_inverse(key, part):
    off_key = jax.random.fold_in(key, 21)
    diag_key = jax.random.fold_in(key, 22)
    raw = jax.random.uniform(off_key, (NSUB, NSUB), jnp.float32)
    symmetric = 0.5 * (raw + raw.T)
    diagonal = jax.random.uniform(diag_key, (NSUB,), jnp.float32, 20.0, 40.0)
    identity = jnp.eye(NSUB, dtype=jnp.float32)
    return (symmetric * (18.0 / NSUB) * (1.0 - identity) + identity * diagonal[:, None]).astype(jnp.bfloat16)


def set_ends(entries, rng, low, top_value):
    extent = entries.shape
    index_at = [jax.random.randint(jax.random.fold_in(rng, axis), (), 0, extent[axis]) for axis in range(len(extent))]
    entries = entries.at[tuple(index_at)].set(low)
    longest = extent.index(max(extent))
    index_at[longest] = (index_at[longest] + 1) % extent[longest]
    return entries.at[tuple(index_at)].set(top_value)


def setup_inputs(seed: int = 0) -> dict:
    splits = jax.random.split(jax.random.key(seed), 5)
    return {
        "rhs": draw_rhs(jax.random.fold_in(splits[4], 71), 0),
        "heights": set_ends(jax.random.randint(splits[1], (NX, NY), 0, NZ // 2), jax.random.fold_in(splits[1], 1), 0, (NZ // 2) - 1).astype(jnp.int32),
        "index_map": jax.random.permutation(splits[2], NSUB).astype(jnp.int32),
        "coarse_inverse": draw_coarse_inverse(jax.random.fold_in(splits[4], 71), 0),
    }


def sine_table(count):
    order = jnp.arange(count, dtype=jnp.float32) + 1.0
    modes = jnp.sqrt(2.0 / (count + 1.0)) * jnp.sin(jnp.pi * order[:, None] * order[None, :] / (count + 1.0))
    values = 2.0 - 2.0 * jnp.cos(jnp.pi * order / (count + 1.0))
    return (modes, values)

def beside_all(array):
    return [array[2:, 1:-1, 1:-1], array[:-2, 1:-1, 1:-1], array[1:-1, 2:, 1:-1], array[1:-1, :-2, 1:-1], array[1:-1, 1:-1, 2:], array[1:-1, 1:-1, :-2]]

def operate(field, fluid):
    solid = 1.0 - fluid
    side = jnp.pad(solid, ((1, 1), (1, 1), (0, 0)))
    bottom = jnp.ones((side.shape[0], side.shape[1], 1), jnp.float32)
    top = jnp.zeros((side.shape[0], side.shape[1], 1), jnp.float32)
    fluid_wide = 1.0 - jnp.concatenate([bottom, side, top], 2)
    padded_field = jnp.pad(field, 1)
    count = jnp.zeros_like(field)
    beside = jnp.zeros_like(field)
    for weight, value in zip(beside_all(fluid_wide), beside_all(padded_field)):
        count = count + weight
        beside = beside + weight * value
    return fluid * (count * field - beside) + solid * field

def modal_blocks(blocks, sine_x, sine_y, sine_z):
    high = lax.Precision.HIGHEST
    section = jnp.einsum('ia,asbk->isbk', sine_x, blocks, precision=high)
    section = jnp.einsum('jb,isbk->isjk', sine_y, section, precision=high)
    return jnp.einsum('kc,isjc->isjk', sine_z, section, precision=high)

def precondition(resid, fluid, index_map, coarse_inverse):
    sine_x, value_x = sine_table(CX + 2)
    sine_y, value_y = sine_table(CY + 2)
    sine_z, value_z = sine_table(NZ)
    inv_eig = 1.0 / (value_x[:, None, None] + value_y[None, :, None] + value_z[None, None, :])
    masked = resid * fluid
    padded = jnp.pad(masked, ((1, 1), (1, 1), (0, 0)))
    column_idx = (jnp.arange(N_GY)[:, None] * CY + jnp.arange(CY + 2)[None, :]).astype(jnp.int32)

    def one_slab(slab_id, totals):
        start = (slab_id * CX).astype(jnp.int32)
        slab = lax.dynamic_slice_in_dim(padded, start, CX + 2, 0)
        blocks = slab[:, column_idx]
        spectral = modal_blocks(blocks, sine_x, sine_y, sine_z) * inv_eig[:, None, :, :]
        solved = modal_blocks(spectral, sine_x, sine_y, sine_z)
        placed = jnp.zeros((CX + 2, NY + 2, NZ), jnp.float32).at[:, column_idx].add(solved)
        before = lax.dynamic_slice_in_dim(totals, start, CX + 2, 0)
        return lax.dynamic_update_slice_in_dim(totals, before + placed, start, 0)
    totals = lax.fori_loop(0, N_GX, one_slab, jnp.zeros((NX + 2, NY + 2, NZ), jnp.float32))
    local = totals[1:-1, 1:-1]
    coarse_res = lax.optimization_barrier(jnp.sum(masked.reshape(N_GX, CX, N_GY, CY, NZ), axis=(1, 3, 4))).reshape(-1) / (CX * CY * NZ)
    coarse_vec = jnp.zeros((NSUB,), jnp.float32).at[index_map].set(coarse_res)
    coarse_sol = jnp.dot(coarse_inverse.astype(jnp.float32), coarse_vec, precision=lax.Precision.HIGHEST)
    picked = coarse_sol[index_map].reshape(N_GX, 1, N_GY, 1, 1)
    spread = jnp.broadcast_to(picked, (N_GX, CX, N_GY, CY, NZ)).reshape(NX, NY, NZ)
    return fluid * (local + spread)

def reference(rhs, heights, index_map, coarse_inverse):
    levels = jnp.arange(NZ).astype(jnp.int32)
    fluid = (levels[None, None, :] >= heights[:, :, None]).astype(jnp.float32)
    source = fluid * rhs
    solution = jnp.zeros_like(source)
    residual = source
    precond = precondition(residual, fluid, index_map, coarse_inverse)
    direction = precond
    energy_now = jnp.sum(residual * precond)
    for iteration in range(ITERS):
        image = operate(direction, fluid)
        step_size = energy_now / jnp.sum(direction * image)
        solution = solution + step_size * direction
        residual = residual - step_size * image
        if iteration + 1 < ITERS:
            precond = precondition(residual, fluid, index_map, coarse_inverse)
            energy_next = jnp.sum(residual * precond)
            direction = precond + energy_next / energy_now * direction
            energy_now = energy_next
    return (solution, residual)
```

```python
import jax
import jax.numpy as jnp
from jax import lax
from jax.sharding import PartitionSpec as P

ITERS = 2


def with_halo(cells, sides, width):
    for axis, dim in sides:
        count = lax.axis_size(axis)
        ends = count - 1
        head = lax.slice_in_dim(cells, 0, width, axis=dim)
        tail = lax.slice_in_dim(cells, cells.shape[dim] - width, cells.shape[dim], axis=dim)
        cells = jnp.concatenate(
            [
                lax.ppermute(tail, axis, [(i, (i + 1) % count) for i in range(ends)]),
                cells,
                lax.ppermute(head, axis, [((i + 1) % count, i) for i in range(ends)]),
            ],
            axis=dim,
        )
    return cells


def exchange(gathered, summed):
    parts = []
    k1 = gathered.shape[0]
    stage = jnp.concatenate([gathered, summed])
    for axis in ("gy", "gx"):
        count = lax.axis_size(axis)
        got = lax.all_to_all(jnp.broadcast_to(stage[None], (count,) + stage.shape), axis, 0, 0, tiled=False)
        width = got.shape[1] - summed.shape[0]
        summed = jnp.sum(got[:, width:], axis=0)
        gathered = got[:, :width].reshape(-1)
        stage = jnp.concatenate([gathered, summed])
    return gathered, summed


def total(value):
    return exchange(jnp.zeros((0,), jnp.float32), value.reshape(1))[1][0]


def extend(field):
    return with_halo(field, (("gx", 0), ("gy", 1)), 1)


def sine_table(count):
    order = jnp.arange(count, dtype=jnp.float32) + 1.0
    modes = jnp.sqrt(2.0 / (count + 1.0)) * jnp.sin(
        jnp.pi * order[:, None] * order[None, :] / (count + 1.0)
    )
    values = 2.0 - 2.0 * jnp.cos(jnp.pi * order / (count + 1.0))
    return (modes, values)


def beside_all(array):
    return [
        array[2:, 1:-1, 1:-1],
        array[:-2, 1:-1, 1:-1],
        array[1:-1, 2:, 1:-1],
        array[1:-1, :-2, 1:-1],
        array[1:-1, 1:-1, 2:],
        array[1:-1, 1:-1, :-2],
    ]


def modal(block, sine_x, sine_y, sine_z):
    high = lax.Precision.HIGHEST
    section = jnp.einsum("ia,abk->ibk", sine_x, block, precision=high)
    section = jnp.einsum("jb,ibk->ijk", sine_y, section, precision=high)
    return jnp.einsum("kc,ijc->ijk", sine_z, section, precision=high)


def margin_sum(block):
    core = block[1:-1, 1:-1]
    rows_x = core.shape[0]
    rows_y = core.shape[1]
    depth = core.shape[2]
    face_x = jnp.concatenate(
        [block[0:1, 1:-1], jnp.zeros((rows_x - 2, rows_y, depth), jnp.float32), block[-1:, 1:-1]], 0
    )
    face_y = jnp.concatenate(
        [block[1:-1, 0:1], jnp.zeros((rows_x, rows_y - 2, depth), jnp.float32), block[1:-1, -1:]], 1
    )
    corner = jnp.zeros_like(core)
    corner = corner.at[0, 0].set(block[0, 0]).at[0, -1].set(block[0, -1])
    corner = corner.at[-1, 0].set(block[-1, 0]).at[-1, -1].set(block[-1, -1])
    arrived = with_halo(jnp.stack([face_x, face_y, corner]), (("gx", 1), ("gy", 2)), 1)
    result = core.at[0].add(arrived[0, 0, 1:-1]).at[-1].add(arrived[0, -1, 1:-1])
    result = result.at[:, 0].add(arrived[1, 1:-1, 0]).at[:, -1].add(arrived[1, 1:-1, -1])
    result = result.at[0, 0].add(arrived[2, 0, 0]).at[0, -1].add(arrived[2, 0, -1])
    result = result.at[-1, 0].add(arrived[2, -1, 0]).at[-1, -1].add(arrived[2, -1, -1])
    return result


def body(rhs, heights, index_map, coarse_inverse):
    rows_x, rows_y, depth = rhs.shape
    subdomains = coarse_inverse.shape[0]
    high = lax.Precision.HIGHEST
    levels = jnp.arange(depth, dtype=jnp.int32)
    solid = (levels[None, None, :] < heights[:, :, None]).astype(jnp.float32)
    fluid = 1.0 - solid
    solid_side = extend(solid)
    bottom = jnp.ones((rows_x + 2, rows_y + 2, 1), jnp.float32)
    top = jnp.zeros((rows_x + 2, rows_y + 2, 1), jnp.float32)
    fluid_wide = 1.0 - jnp.concatenate([bottom, solid_side, top], 2)
    count = jnp.zeros_like(fluid)
    for weight in beside_all(fluid_wide):
        count = count + weight
    sine_x, value_x = sine_table(rows_x + 2)
    sine_y, value_y = sine_table(rows_y + 2)
    sine_z, value_z = sine_table(depth)
    inv_eig = 1.0 / (value_x[:, None, None] + value_y[None, :, None] + value_z[None, None, :])
    my_slot = lax.dynamic_index_in_dim(index_map, lax.axis_index(("gx", "gy")), 0, keepdims=False)
    inverse_row = lax.dynamic_index_in_dim(coarse_inverse, my_slot, 0, keepdims=False).astype(
        jnp.float32
    )
    picked_row = inverse_row[index_map]

    def precondition(resid):
        masked = resid * fluid
        wide = extend(masked)
        spectral = modal(wide, sine_x, sine_y, sine_z) * inv_eig
        local = margin_sum(modal(spectral, sine_x, sine_y, sine_z))
        coarse_res = jnp.sum(masked) / (rows_x * rows_y * depth)
        every = exchange(coarse_res.reshape(1), jnp.zeros((0,), jnp.float32))[0]
        coarse_value = jnp.sum(picked_row * every)
        return fluid * (local + coarse_value)

    def energy_sum(resid, precond):
        return total(jnp.sum(resid * precond))

    source = fluid * rhs
    solution = jnp.zeros_like(source)
    residual = source
    precond = precondition(residual)
    direction = precond
    energy_now = energy_sum(residual, precond)
    for iteration in range(ITERS):
        operate_wide = extend(direction)
        padded_field = jnp.pad(operate_wide, ((0, 0), (0, 0), (1, 1)))
        beside = jnp.zeros_like(direction)
        for operate_weight, value in zip(beside_all(fluid_wide), beside_all(padded_field)):
            beside = beside + operate_weight * value
        image = fluid * (count * direction - beside) + solid * direction
        step_size = energy_now / total(jnp.sum(direction * image))
        solution = solution + step_size * direction
        residual = residual - step_size * image
        if iteration + 1 < ITERS:
            precond = precondition(residual)
            energy_next = energy_sum(residual, precond)
            direction = precond + energy_next / energy_now * direction
            energy_now = energy_next
    return (solution, residual)


def solution(mesh):
    in_specs = (P("gx", "gy", None), P("gx", "gy"), P(), P())
    out_specs = (P("gx", "gy", None), P("gx", "gy", None))
    return jax.shard_map(body, mesh=mesh, in_specs=in_specs, out_specs=out_specs, check_vma=False)
```

```python
import jax
import jax.numpy as jnp
from jax import lax
from jax.sharding import PartitionSpec as P

ITERS = 2


def with_halo(cells, sides, width):
    for axis, dim in sides:
        count = lax.axis_size(axis)
        ends = count - 1
        head = lax.slice_in_dim(cells, 0, width, axis=dim)
        tail = lax.slice_in_dim(cells, cells.shape[dim] - width, cells.shape[dim], axis=dim)
        cells = jnp.concatenate(
            [
                lax.ppermute(tail, axis, [(i, (i + 1) % count) for i in range(ends)]),
                cells,
                lax.ppermute(head, axis, [((i + 1) % count, i) for i in range(ends)]),
            ],
            axis=dim,
        )
    return cells


def exchange(gathered, summed):
    parts = []
    k1 = gathered.shape[0]
    stage = jnp.concatenate([gathered, summed])
    for axis in ("gy", "gx"):
        count = lax.axis_size(axis)
        got = lax.all_to_all(jnp.broadcast_to(stage[None], (count,) + stage.shape), axis, 0, 0, tiled=False)
        width = got.shape[1] - summed.shape[0]
        summed = jnp.sum(got[:, width:], axis=0)
        gathered = got[:, :width].reshape(-1)
        stage = jnp.concatenate([gathered, summed])
    return gathered, summed


def total(value):
    return exchange(jnp.zeros((0,), jnp.float32), value.reshape(1))[1][0]


def extend(field):
    return with_halo(field, (("gx", 0), ("gy", 1)), 1)


def sine_table(count):
    order = jnp.arange(count, dtype=jnp.float32) + 1.0
    modes = jnp.sqrt(2.0 / (count + 1.0)) * jnp.sin(
        jnp.pi * order[:, None] * order[None, :] / (count + 1.0)
    )
    values = 2.0 - 2.0 * jnp.cos(jnp.pi * order / (count + 1.0))
    return (modes, values)


def beside_all(array):
    return [
        array[2:, 1:-1, 1:-1],
        array[:-2, 1:-1, 1:-1],
        array[1:-1, 2:, 1:-1],
        array[1:-1, :-2, 1:-1],
        array[1:-1, 1:-1, 2:],
        array[1:-1, 1:-1, :-2],
    ]


def modal(block, sine_x, sine_y, sine_z):
    high = lax.Precision.HIGHEST
    section = jnp.einsum("ia,abk->ibk", sine_x, block, precision=high)
    section = jnp.einsum("jb,ibk->ijk", sine_y, section, precision=high)
    return jnp.einsum("kc,ijc->ijk", sine_z, section, precision=high)


def margin_sum(block):
    core = block[1:-1, 1:-1]
    rows_x = core.shape[0]
    rows_y = core.shape[1]
    depth = core.shape[2]
    face_x = jnp.concatenate(
        [block[0:1, 1:-1], jnp.zeros((rows_x - 2, rows_y, depth), jnp.float32), block[-1:, 1:-1]], 0
    )
    face_y = jnp.concatenate(
        [block[1:-1, 0:1], jnp.zeros((rows_x, rows_y - 2, depth), jnp.float32), block[1:-1, -1:]], 1
    )
    corner = jnp.zeros_like(core)
    corner = corner.at[0, 0].set(block[0, 0]).at[0, -1].set(block[0, -1])
    corner = corner.at[-1, 0].set(block[-1, 0]).at[-1, -1].set(block[-1, -1])
    arrived = with_halo(jnp.stack([face_x, face_y, corner]), (("gx", 1), ("gy", 2)), 1)
    result = core.at[0].add(arrived[0, 0, 1:-1]).at[-1].add(arrived[0, -1, 1:-1])
    result = result.at[:, 0].add(arrived[1, 1:-1, 0]).at[:, -1].add(arrived[1, 1:-1, -1])
    result = result.at[0, 0].add(arrived[2, 0, 0]).at[0, -1].add(arrived[2, 0, -1])
    result = result.at[-1, 0].add(arrived[2, -1, 0]).at[-1, -1].add(arrived[2, -1, -1])
    return result


def face_halo(cells):
    count_x = lax.axis_size("gx")
    count_y = lax.axis_size("gy")
    up_x = [(i, i + 1) for i in range(count_x - 1)]
    down_x = [(i + 1, i) for i in range(count_x - 1)]
    up_y = [(i, i + 1) for i in range(count_y - 1)]
    down_y = [(i + 1, i) for i in range(count_y - 1)]
    low_x = lax.ppermute(cells[-1:], "gx", up_x)
    high_x = lax.ppermute(cells[:1], "gx", down_x)
    low_y = lax.ppermute(cells[:, -1:], "gy", up_y)
    high_y = lax.ppermute(cells[:, :1], "gy", down_y)
    middle = jnp.concatenate([low_y, cells, high_y], axis=1)
    pad_y = ((0, 0), (1, 1), (0, 0))
    return jnp.concatenate([jnp.pad(low_x, pad_y), middle, jnp.pad(high_x, pad_y)], axis=0)


def body(rhs, heights, index_map, coarse_inverse):
    rows_x, rows_y, depth = rhs.shape
    subdomains = coarse_inverse.shape[0]
    cells = rows_x * rows_y * depth
    high = lax.Precision.HIGHEST
    levels = jnp.arange(depth, dtype=jnp.int32)
    solid = (levels[None, None, :] < heights[:, :, None]).astype(jnp.float32)
    fluid = 1.0 - solid
    solid_side = extend(solid)
    bottom = jnp.ones((rows_x + 2, rows_y + 2, 1), jnp.float32)
    top = jnp.zeros((rows_x + 2, rows_y + 2, 1), jnp.float32)
    fluid_wide = 1.0 - jnp.concatenate([bottom, solid_side, top], 2)
    count = jnp.zeros_like(fluid)
    for weight in beside_all(fluid_wide):
        count = count + weight
    sine_x, value_x = sine_table(rows_x + 2)
    sine_y, value_y = sine_table(rows_y + 2)
    sine_z, value_z = sine_table(depth)
    inv_eig = 1.0 / (value_x[:, None, None] + value_y[None, :, None] + value_z[None, None, :])
    my_slot = lax.dynamic_index_in_dim(index_map, lax.axis_index(("gx", "gy")), 0, keepdims=False)
    inverse = coarse_inverse.astype(jnp.float32)
    none = jnp.zeros((0,), jnp.float32)

    def local_solve(masked):
        wide = extend(masked)
        spectral = modal(wide, sine_x, sine_y, sine_z) * inv_eig
        return margin_sum(modal(spectral, sine_x, sine_y, sine_z))

    def coarse(gathered):
        vec = jnp.zeros((subdomains,), jnp.float32).at[index_map].set(gathered)
        sol = jnp.dot(inverse, vec, precision=high)
        return vec, sol, lax.dynamic_index_in_dim(sol, my_slot, 0, keepdims=False)

    def operate(direction):
        padded_field = jnp.pad(face_halo(direction), ((0, 0), (0, 0), (1, 1)))
        beside = jnp.zeros_like(direction)
        for operate_weight, value in zip(beside_all(fluid_wide), beside_all(padded_field)):
            beside = beside + operate_weight * value
        return fluid * (count * direction - beside) + solid * direction

    residual = fluid * rhs
    masked = residual * fluid
    local0 = local_solve(masked)
    every, partial = exchange(
        (jnp.sum(masked) / cells).reshape(1), jnp.sum(residual * fluid * local0).reshape(1)
    )
    vec0, sol0, value0 = coarse(every)
    energy_now = partial[0] + cells * jnp.sum(vec0 * sol0)
    precond = fluid * (local0 + value0)
    direction = precond

    image = operate(direction)
    masked_w = image * fluid
    local_w = local_solve(masked_w)
    every_w, partial = exchange(
        (jnp.sum(masked_w) / cells).reshape(1),
        jnp.stack(
            [
                jnp.sum(direction * image),
                jnp.sum(residual * fluid * local_w),
                jnp.sum(image * fluid * local0),
                jnp.sum(image * fluid * local_w),
            ]
        ),
    )
    vec_w, sol_w, value_w = coarse(every_w)
    step_size = energy_now / partial[0]
    solution = step_size * direction
    residual = residual - step_size * image
    cross_r = partial[1] + cells * jnp.sum(vec0 * sol_w)
    cross_w = partial[2] + cells * jnp.sum(vec_w * sol0)
    square_w = partial[3] + cells * jnp.sum(vec_w * sol_w)
    energy_next = energy_now - step_size * (cross_r + cross_w) + step_size * step_size * square_w
    precond = precond - step_size * (fluid * (local_w + value_w))
    direction = precond + energy_next / energy_now * direction

    image = operate(direction)
    step_size = energy_next / total(jnp.sum(direction * image))
    solution = solution + step_size * direction
    residual = residual - step_size * image
    return (solution, residual)


def solution(mesh):
    in_specs = (P("gx", "gy", None), P("gx", "gy"), P(), P())
    out_specs = (P("gx", "gy", None), P("gx", "gy", None))
    return jax.shard_map(body, mesh=mesh, in_specs=in_specs, out_specs=out_specs, check_vma=False)
```

```python
import jax
import jax.numpy as jnp
from jax import lax
from jax.sharding import PartitionSpec as P

ITERS = 2


def with_halo(cells, sides, width):
    for axis, dim in sides:
        count = lax.axis_size(axis)
        ends = count - 1
        head = lax.slice_in_dim(cells, 0, width, axis=dim)
        tail = lax.slice_in_dim(cells, cells.shape[dim] - width, cells.shape[dim], axis=dim)
        cells = jnp.concatenate(
            [
                lax.ppermute(tail, axis, [(i, (i + 1) % count) for i in range(ends)]),
                cells,
                lax.ppermute(head, axis, [((i + 1) % count, i) for i in range(ends)]),
            ],
            axis=dim,
        )
    return cells


def exchange(gathered, summed):
    parts = []
    k1 = gathered.shape[0]
    stage = jnp.concatenate([gathered, summed])
    for axis in ("gy", "gx"):
        count = lax.axis_size(axis)
        got = lax.all_to_all(jnp.broadcast_to(stage[None], (count,) + stage.shape), axis, 0, 0, tiled=False)
        width = got.shape[1] - summed.shape[0]
        summed = jnp.sum(got[:, width:], axis=0)
        gathered = got[:, :width].reshape(-1)
        stage = jnp.concatenate([gathered, summed])
    return gathered, summed


def total(value):
    return exchange(jnp.zeros((0,), jnp.float32), value.reshape(1))[1][0]


def extend(field):
    return with_halo(field, (("gx", 0), ("gy", 1)), 1)


def sine_table(count):
    order = jnp.arange(count, dtype=jnp.float32) + 1.0
    modes = jnp.sqrt(2.0 / (count + 1.0)) * jnp.sin(
        jnp.pi * order[:, None] * order[None, :] / (count + 1.0)
    )
    values = 2.0 - 2.0 * jnp.cos(jnp.pi * order / (count + 1.0))
    return (modes, values)


def beside_all(array):
    return [
        array[2:, 1:-1, 1:-1],
        array[:-2, 1:-1, 1:-1],
        array[1:-1, 2:, 1:-1],
        array[1:-1, :-2, 1:-1],
        array[1:-1, 1:-1, 2:],
        array[1:-1, 1:-1, :-2],
    ]


def modal(block, sine_x, sine_y, sine_z):
    high = lax.Precision.HIGHEST
    section = jnp.einsum("ia,abk->ibk", sine_x, block, precision=high)
    section = jnp.einsum("jb,ibk->ijk", sine_y, section, precision=high)
    return jnp.einsum("kc,ijc->ijk", sine_z, section, precision=high)


def margin_sum(block):
    count_x = lax.axis_size("gx")
    count_y = lax.axis_size("gy")
    up_x = [(i, i + 1) for i in range(count_x - 1)]
    down_x = [(i + 1, i) for i in range(count_x - 1)]
    up_y = [(i, i + 1) for i in range(count_y - 1)]
    down_y = [(i + 1, i) for i in range(count_y - 1)]
    rows_x = block.shape[0] - 2
    rows_y = block.shape[1] - 2
    from_low = lax.ppermute(block[-1:], "gx", up_x)
    from_high = lax.ppermute(block[:1], "gx", down_x)
    body_rows = block[1:-1]
    body_rows = body_rows + jnp.pad(from_low, ((0, rows_x - 1), (0, 0), (0, 0)))
    body_rows = body_rows + jnp.pad(from_high, ((rows_x - 1, 0), (0, 0), (0, 0)))
    from_left = lax.ppermute(body_rows[:, -1:], "gy", up_y)
    from_right = lax.ppermute(body_rows[:, :1], "gy", down_y)
    core = body_rows[:, 1:-1]
    core = core + jnp.pad(from_left, ((0, 0), (0, rows_y - 1), (0, 0)))
    core = core + jnp.pad(from_right, ((0, 0), (rows_y - 1, 0), (0, 0)))
    return core


def face_halo(cells):
    count_x = lax.axis_size("gx")
    count_y = lax.axis_size("gy")
    up_x = [(i, i + 1) for i in range(count_x - 1)]
    down_x = [(i + 1, i) for i in range(count_x - 1)]
    up_y = [(i, i + 1) for i in range(count_y - 1)]
    down_y = [(i + 1, i) for i in range(count_y - 1)]
    low_x = lax.ppermute(cells[-1:], "gx", up_x)
    high_x = lax.ppermute(cells[:1], "gx", down_x)
    low_y = lax.ppermute(cells[:, -1:], "gy", up_y)
    high_y = lax.ppermute(cells[:, :1], "gy", down_y)
    middle = jnp.concatenate([low_y, cells, high_y], axis=1)
    pad_y = ((0, 0), (1, 1), (0, 0))
    return jnp.concatenate([jnp.pad(low_x, pad_y), middle, jnp.pad(high_x, pad_y)], axis=0)


def body(rhs, heights, index_map, coarse_inverse):
    rows_x, rows_y, depth = rhs.shape
    subdomains = coarse_inverse.shape[0]
    cells = rows_x * rows_y * depth
    high = lax.Precision.HIGHEST
    levels = jnp.arange(depth, dtype=jnp.int32)
    solid = (levels[None, None, :] < heights[:, :, None]).astype(jnp.float32)
    fluid = 1.0 - solid
    residual = fluid * rhs
    masked = residual * fluid
    both_wide = extend(jnp.concatenate([masked, solid], axis=2))
    solid_side = both_wide[:, :, depth:]
    bottom = jnp.ones((rows_x + 2, rows_y + 2, 1), jnp.float32)
    top = jnp.zeros((rows_x + 2, rows_y + 2, 1), jnp.float32)
    fluid_wide = 1.0 - jnp.concatenate([bottom, solid_side, top], 2)
    count = jnp.zeros_like(fluid)
    for weight in beside_all(fluid_wide):
        count = count + weight
    sine_x, value_x = sine_table(rows_x + 2)
    sine_y, value_y = sine_table(rows_y + 2)
    sine_z, value_z = sine_table(depth)
    inv_eig = 1.0 / (value_x[:, None, None] + value_y[None, :, None] + value_z[None, None, :])
    my_slot = lax.dynamic_index_in_dim(index_map, lax.axis_index(("gx", "gy")), 0, keepdims=False)
    inverse = coarse_inverse.astype(jnp.float32)
    none = jnp.zeros((0,), jnp.float32)

    def local_solve(masked, wide=None):
        if wide is None:
            wide = extend(masked)
        spectral = modal(wide, sine_x, sine_y, sine_z) * inv_eig
        return margin_sum(modal(spectral, sine_x, sine_y, sine_z))

    def coarse(gathered):
        vec = jnp.zeros((subdomains,), jnp.float32).at[index_map].set(gathered)
        sol = jnp.dot(inverse, vec, precision=high)
        return vec, sol, lax.dynamic_index_in_dim(sol, my_slot, 0, keepdims=False)

    def operate(direction):
        padded_field = jnp.pad(face_halo(direction), ((0, 0), (0, 0), (1, 1)))
        beside = jnp.zeros_like(direction)
        for operate_weight, value in zip(beside_all(fluid_wide), beside_all(padded_field)):
            beside = beside + operate_weight * value
        return fluid * (count * direction - beside) + solid * direction

    local0 = local_solve(masked, both_wide[:, :, :depth])
    every, partial = exchange(
        (jnp.sum(masked) / cells).reshape(1), jnp.sum(residual * fluid * local0).reshape(1)
    )
    vec0, sol0, value0 = coarse(every)
    energy_now = partial[0] + cells * jnp.sum(vec0 * sol0)
    precond = fluid * (local0 + value0)
    direction = precond

    image = operate(direction)
    masked_w = image * fluid
    local_w = local_solve(masked_w)
    every_w, partial = exchange(
        (jnp.sum(masked_w) / cells).reshape(1),
        jnp.stack(
            [
                jnp.sum(direction * image),
                jnp.sum(residual * fluid * local_w),
                jnp.sum(image * fluid * local0),
                jnp.sum(image * fluid * local_w),
            ]
        ),
    )
    vec_w, sol_w, value_w = coarse(every_w)
    step_size = energy_now / partial[0]
    solution = step_size * direction
    residual = residual - step_size * image
    cross_r = partial[1] + cells * jnp.sum(vec0 * sol_w)
    cross_w = partial[2] + cells * jnp.sum(vec_w * sol0)
    square_w = partial[3] + cells * jnp.sum(vec_w * sol_w)
    energy_next = energy_now - step_size * (cross_r + cross_w) + step_size * step_size * square_w
    precond = precond - step_size * (fluid * (local_w + value_w))
    direction = precond + energy_next / energy_now * direction

    image = operate(direction)
    step_size = energy_next / total(jnp.sum(direction * image))
    solution = solution + step_size * direction
    residual = residual - step_size * image
    return (solution, residual)


def solution(mesh):
    in_specs = (P("gx", "gy", None), P("gx", "gy"), P(), P())
    out_specs = (P("gx", "gy", None), P("gx", "gy", None))
    return jax.shard_map(body, mesh=mesh, in_specs=in_specs, out_specs=out_specs, check_vma=False)
```

```python
import jax
import jax.numpy as jnp
from jax import lax
from jax.sharding import PartitionSpec as P

ITERS = 2


def with_halo(cells, sides, width):
    for axis, dim in sides:
        count = lax.axis_size(axis)
        ends = count - 1
        head = lax.slice_in_dim(cells, 0, width, axis=dim)
        tail = lax.slice_in_dim(cells, cells.shape[dim] - width, cells.shape[dim], axis=dim)
        cells = jnp.concatenate(
            [
                lax.ppermute(tail, axis, [(i, (i + 1) % count) for i in range(ends)]),
                cells,
                lax.ppermute(head, axis, [((i + 1) % count, i) for i in range(ends)]),
            ],
            axis=dim,
        )
    return cells


def exchange(gathered, summed):
    parts = []
    k1 = gathered.shape[0]
    stage = jnp.concatenate([gathered, summed])
    for axis in ("gy", "gx"):
        count = lax.axis_size(axis)
        got = lax.all_to_all(jnp.broadcast_to(stage[None], (count,) + stage.shape), axis, 0, 0, tiled=False)
        width = got.shape[1] - summed.shape[0]
        summed = jnp.sum(got[:, width:], axis=0)
        gathered = got[:, :width].reshape(-1)
        stage = jnp.concatenate([gathered, summed])
    return gathered, summed


def total(value):
    return exchange(jnp.zeros((0,), jnp.float32), value.reshape(1))[1][0]


def extend(field):
    return with_halo(field, (("gx", 0), ("gy", 1)), 1)


def sine_table(count):
    order = jnp.arange(count, dtype=jnp.float32) + 1.0
    modes = jnp.sqrt(2.0 / (count + 1.0)) * jnp.sin(
        jnp.pi * order[:, None] * order[None, :] / (count + 1.0)
    )
    values = 2.0 - 2.0 * jnp.cos(jnp.pi * order / (count + 1.0))
    return (modes, values)


def beside_all(array):
    return [
        array[2:, 1:-1, 1:-1],
        array[:-2, 1:-1, 1:-1],
        array[1:-1, 2:, 1:-1],
        array[1:-1, :-2, 1:-1],
        array[1:-1, 1:-1, 2:],
        array[1:-1, 1:-1, :-2],
    ]


def modal(block, sine_x, sine_y, sine_z):
    high = lax.Precision.HIGHEST
    section = jnp.einsum("ia,abk->ibk", sine_x, block, precision=high)
    section = jnp.einsum("jb,ibk->ijk", sine_y, section, precision=high)
    return jnp.einsum("kc,ijc->ijk", sine_z, section, precision=high)


def margin_sum(block):
    count_x = lax.axis_size("gx")
    count_y = lax.axis_size("gy")
    up_x = [(i, i + 1) for i in range(count_x - 1)]
    down_x = [(i + 1, i) for i in range(count_x - 1)]
    up_y = [(i, i + 1) for i in range(count_y - 1)]
    down_y = [(i + 1, i) for i in range(count_y - 1)]
    rows_x = block.shape[0] - 2
    rows_y = block.shape[1] - 2
    from_low = lax.ppermute(block[-1:], "gx", up_x)
    from_high = lax.ppermute(block[:1], "gx", down_x)
    body_rows = block[1:-1]
    body_rows = body_rows + jnp.pad(from_low, ((0, rows_x - 1), (0, 0), (0, 0)))
    body_rows = body_rows + jnp.pad(from_high, ((rows_x - 1, 0), (0, 0), (0, 0)))
    from_left = lax.ppermute(body_rows[:, -1:], "gy", up_y)
    from_right = lax.ppermute(body_rows[:, :1], "gy", down_y)
    core = body_rows[:, 1:-1]
    core = core + jnp.pad(from_left, ((0, 0), (0, rows_y - 1), (0, 0)))
    core = core + jnp.pad(from_right, ((0, 0), (rows_y - 1, 0), (0, 0)))
    return core


def face_halo(cells):
    count_x = lax.axis_size("gx")
    count_y = lax.axis_size("gy")
    up_x = [(i, i + 1) for i in range(count_x - 1)]
    down_x = [(i + 1, i) for i in range(count_x - 1)]
    up_y = [(i, i + 1) for i in range(count_y - 1)]
    down_y = [(i + 1, i) for i in range(count_y - 1)]
    low_x = lax.ppermute(cells[-1:], "gx", up_x)
    high_x = lax.ppermute(cells[:1], "gx", down_x)
    low_y = lax.ppermute(cells[:, -1:], "gy", up_y)
    high_y = lax.ppermute(cells[:, :1], "gy", down_y)
    middle = jnp.concatenate([low_y, cells, high_y], axis=1)
    pad_y = ((0, 0), (1, 1), (0, 0))
    return jnp.concatenate([jnp.pad(low_x, pad_y), middle, jnp.pad(high_x, pad_y)], axis=0)


def body(rhs, heights, index_map, coarse_inverse):
    rows_x, rows_y, depth = rhs.shape
    subdomains = coarse_inverse.shape[0]
    cells = rows_x * rows_y * depth
    high = lax.Precision.HIGHEST
    levels = jnp.arange(depth, dtype=jnp.int32)
    solid = (levels[None, None, :] < heights[:, :, None]).astype(jnp.float32)
    fluid = 1.0 - solid
    residual = fluid * rhs
    masked = residual * fluid
    both_wide = extend(jnp.concatenate([masked, solid], axis=2))
    solid_side = both_wide[:, :, depth:]
    bottom = jnp.ones((rows_x + 2, rows_y + 2, 1), jnp.float32)
    top = jnp.zeros((rows_x + 2, rows_y + 2, 1), jnp.float32)
    fluid_wide = 1.0 - jnp.concatenate([bottom, solid_side, top], 2)
    count = jnp.zeros_like(fluid)
    for weight in beside_all(fluid_wide):
        count = count + weight
    sine_x, value_x = sine_table(rows_x + 2)
    sine_y, value_y = sine_table(rows_y + 2)
    sine_z, value_z = sine_table(depth)
    inv_eig = 1.0 / (value_x[:, None, None] + value_y[None, :, None] + value_z[None, None, :])
    my_slot = lax.dynamic_index_in_dim(index_map, lax.axis_index(("gx", "gy")), 0, keepdims=False)
    inverse = coarse_inverse.astype(jnp.float32)
    count_x = lax.axis_size("gx")
    count_y = lax.axis_size("gy")

    def local_solve(masked, wide=None):
        if wide is None:
            wide = extend(masked)
        spectral = modal(wide, sine_x, sine_y, sine_z) * inv_eig
        return margin_sum(modal(spectral, sine_x, sine_y, sine_z))

    def coarse(gathered):
        vec = jnp.zeros((subdomains,), jnp.float32).at[index_map].set(gathered)
        sol = jnp.dot(inverse, vec, precision=high)
        return vec, sol, lax.dynamic_index_in_dim(sol, my_slot, 0, keepdims=False)

    def operate(direction, wide=None):
        if wide is None:
            wide = face_halo(direction)
        padded_field = jnp.pad(wide, ((0, 0), (0, 0), (1, 1)))
        beside = jnp.zeros_like(direction)
        for operate_weight, value in zip(beside_all(fluid_wide), beside_all(padded_field)):
            beside = beside + operate_weight * value
        return fluid * (count * direction - beside) + solid * direction

    inner = fluid_wide[:, :, 1:-1]
    k_row = jnp.stack(
        [
            jnp.sum(fluid * operate(fluid, jnp.pad(fluid, ((1, 1), (1, 1), (0, 0))))),
            -jnp.sum(fluid[0] * inner[0, 1:-1]),
            -jnp.sum(fluid[-1] * inner[-1, 1:-1]),
            -jnp.sum(fluid[:, 0] * inner[1:-1, 0]),
            -jnp.sum(fluid[:, -1] * inner[1:-1, -1]),
        ]
    )

    local0 = local_solve(masked, both_wide[:, :, :depth])
    every, partial = exchange(
        jnp.concatenate([(jnp.sum(masked) / cells).reshape(1), k_row]),
        jnp.sum(residual * fluid * local0).reshape(1),
    )
    every = every.reshape(subdomains, 6)
    k_grid = every[:, 1:].reshape(count_x, count_y, 5)
    vec0, sol0, value0 = coarse(every[:, 0])
    energy_now = partial[0] + cells * jnp.sum(vec0 * sol0)
    precond = fluid * (local0 + value0)
    direction = precond

    image = operate(direction)
    masked_w = image * fluid
    local_w = local_solve(masked_w)
    fluid_local_w = fluid * local_w
    image_local_w = operate(fluid_local_w)
    every_w, partial = exchange(
        jnp.stack([jnp.sum(masked_w) / cells, jnp.sum(fluid * image_local_w)]),
        jnp.stack(
            [
                jnp.sum(direction * image),
                jnp.sum(residual * fluid * local_w),
                jnp.sum(image * fluid * local0),
                jnp.sum(image * fluid * local_w),
                jnp.sum(fluid_local_w * image_local_w),
            ]
        ),
    )
    every_w = every_w.reshape(subdomains, 2)
    vec_w, sol_w, value_w = coarse(every_w[:, 0])
    delta_now = partial[0]
    step_size = energy_now / delta_now
    solution = step_size * direction
    residual = residual - step_size * image
    cross_r = partial[1] + cells * jnp.sum(vec0 * sol_w)
    cross_w = partial[2] + cells * jnp.sum(vec_w * sol0)
    square_w = partial[3] + cells * jnp.sum(vec_w * sol_w)
    energy_next = energy_now - step_size * (cross_r + cross_w) + step_size * step_size * square_w
    ratio = energy_next / energy_now
    precond = precond - step_size * (fluid * (local_w + value_w))
    direction = precond + ratio * direction

    coarse_w = sol_w[index_map]
    grid_w = coarse_w.reshape(count_x, count_y)
    near_w = jnp.stack(
        [
            grid_w,
            jnp.pad(grid_w[:-1], ((1, 0), (0, 0))),
            jnp.pad(grid_w[1:], ((0, 1), (0, 0))),
            jnp.pad(grid_w[:, :-1], ((0, 0), (1, 0))),
            jnp.pad(grid_w[:, 1:], ((0, 0), (0, 1))),
        ],
        axis=-1,
    )
    coarse_energy = jnp.sum(grid_w[:, :, None] * k_grid * near_w)
    square_m = partial[4] + 2.0 * jnp.sum(coarse_w * every_w[:, 1]) + coarse_energy
    grow = 1.0 + ratio
    delta_next = grow * grow * delta_now - 2.0 * step_size * grow * square_w + step_size * step_size * square_m

    mine = near_w[lax.axis_index("gx"), lax.axis_index("gy")]
    coarse_wide = jnp.zeros((rows_x + 2, rows_y + 2, depth), jnp.float32)
    coarse_wide = coarse_wide.at[1:-1, 1:-1].set(fluid * mine[0])
    coarse_wide = coarse_wide.at[0, 1:-1].set(inner[0, 1:-1] * mine[1])
    coarse_wide = coarse_wide.at[-1, 1:-1].set(inner[-1, 1:-1] * mine[2])
    coarse_wide = coarse_wide.at[1:-1, 0].set(inner[1:-1, 0] * mine[3])
    coarse_wide = coarse_wide.at[1:-1, -1].set(inner[1:-1, -1] * mine[4])
    image_m = image_local_w + operate(fluid * mine[0], coarse_wide)
    image = grow * image - step_size * image_m

    step_size = energy_next / delta_next
    solution = solution + step_size * direction
    residual = residual - step_size * image
    return (solution, residual)


def solution(mesh):
    in_specs = (P("gx", "gy", None), P("gx", "gy"), P(), P())
    out_specs = (P("gx", "gy", None), P("gx", "gy", None))
    return jax.shard_map(body, mesh=mesh, in_specs=in_specs, out_specs=out_specs, check_vma=False)
```

```python
import jax
import jax.numpy as jnp
from jax import lax
from jax.sharding import PartitionSpec as P

ITERS = 2


def with_halo(cells, sides, width):
    for axis, dim in sides:
        count = lax.axis_size(axis)
        ends = count - 1
        head = lax.slice_in_dim(cells, 0, width, axis=dim)
        tail = lax.slice_in_dim(cells, cells.shape[dim] - width, cells.shape[dim], axis=dim)
        cells = jnp.concatenate(
            [
                lax.ppermute(tail, axis, [(i, (i + 1) % count) for i in range(ends)]),
                cells,
                lax.ppermute(head, axis, [((i + 1) % count, i) for i in range(ends)]),
            ],
            axis=dim,
        )
    return cells


def exchange(gathered, summed):
    parts = []
    k1 = gathered.shape[0]
    stage = jnp.concatenate([gathered, summed])
    for axis in ("gy", "gx"):
        count = lax.axis_size(axis)
        got = lax.all_to_all(jnp.broadcast_to(stage[None], (count,) + stage.shape), axis, 0, 0, tiled=False)
        width = got.shape[1] - summed.shape[0]
        summed = jnp.sum(got[:, width:], axis=0)
        gathered = got[:, :width].reshape(-1)
        stage = jnp.concatenate([gathered, summed])
    return gathered, summed


def total(value):
    return exchange(jnp.zeros((0,), jnp.float32), value.reshape(1))[1][0]


def extend(field):
    return with_halo(field, (("gx", 0), ("gy", 1)), 1)


def sine_table(count):
    order = jnp.arange(count, dtype=jnp.float32) + 1.0
    modes = jnp.sqrt(2.0 / (count + 1.0)) * jnp.sin(
        jnp.pi * order[:, None] * order[None, :] / (count + 1.0)
    )
    values = 2.0 - 2.0 * jnp.cos(jnp.pi * order / (count + 1.0))
    return (modes, values)


def beside_all(array):
    return [
        array[2:, 1:-1, 1:-1],
        array[:-2, 1:-1, 1:-1],
        array[1:-1, 2:, 1:-1],
        array[1:-1, :-2, 1:-1],
        array[1:-1, 1:-1, 2:],
        array[1:-1, 1:-1, :-2],
    ]


def modal(block, sine_x, sine_y, sine_z):
    high = lax.Precision.HIGHEST
    section = jnp.einsum("ia,abk->ibk", sine_x, block, precision=high)
    section = jnp.einsum("jb,ibk->ijk", sine_y, section, precision=high)
    return jnp.einsum("kc,ijc->ijk", sine_z, section, precision=high)


def margin_sum(block):
    count_x = lax.axis_size("gx")
    count_y = lax.axis_size("gy")
    up_x = [(i, i + 1) for i in range(count_x - 1)]
    down_x = [(i + 1, i) for i in range(count_x - 1)]
    up_y = [(i, i + 1) for i in range(count_y - 1)]
    down_y = [(i + 1, i) for i in range(count_y - 1)]
    rows_x = block.shape[0] - 2
    rows_y = block.shape[1] - 2
    from_low = lax.ppermute(block[-1:], "gx", up_x)
    from_high = lax.ppermute(block[:1], "gx", down_x)
    body_rows = block[1:-1]
    body_rows = body_rows + jnp.pad(from_low, ((0, rows_x - 1), (0, 0), (0, 0)))
    body_rows = body_rows + jnp.pad(from_high, ((rows_x - 1, 0), (0, 0), (0, 0)))
    from_left = lax.ppermute(body_rows[:, -1:], "gy", up_y)
    from_right = lax.ppermute(body_rows[:, :1], "gy", down_y)
    core = body_rows[:, 1:-1]
    core = core + jnp.pad(from_left, ((0, 0), (0, rows_y - 1), (0, 0)))
    core = core + jnp.pad(from_right, ((0, 0), (rows_y - 1, 0), (0, 0)))
    return core


def face_halo(cells):
    count_x = lax.axis_size("gx")
    count_y = lax.axis_size("gy")
    up_x = [(i, i + 1) for i in range(count_x - 1)]
    down_x = [(i + 1, i) for i in range(count_x - 1)]
    up_y = [(i, i + 1) for i in range(count_y - 1)]
    down_y = [(i + 1, i) for i in range(count_y - 1)]
    low_x = lax.ppermute(cells[-1:], "gx", up_x)
    high_x = lax.ppermute(cells[:1], "gx", down_x)
    low_y = lax.ppermute(cells[:, -1:], "gy", up_y)
    high_y = lax.ppermute(cells[:, :1], "gy", down_y)
    middle = jnp.concatenate([low_y, cells, high_y], axis=1)
    pad_y = ((0, 0), (1, 1), (0, 0))
    return jnp.concatenate([jnp.pad(low_x, pad_y), middle, jnp.pad(high_x, pad_y)], axis=0)


def body(rhs, heights, index_map, coarse_inverse):
    rows_x, rows_y, depth = rhs.shape
    subdomains = coarse_inverse.shape[0]
    cells = rows_x * rows_y * depth
    high = lax.Precision.HIGHEST
    levels = jnp.arange(depth, dtype=jnp.int32)
    solid = (levels[None, None, :] < heights[:, :, None]).astype(jnp.float32)
    fluid = 1.0 - solid
    residual = fluid * rhs
    masked = residual * fluid
    both_wide = extend(jnp.concatenate([masked, solid], axis=2))
    solid_side = both_wide[:, :, depth:]
    bottom = jnp.ones((rows_x + 2, rows_y + 2, 1), jnp.float32)
    top = jnp.zeros((rows_x + 2, rows_y + 2, 1), jnp.float32)
    fluid_wide = 1.0 - jnp.concatenate([bottom, solid_side, top], 2)
    count = jnp.zeros_like(fluid)
    for weight in beside_all(fluid_wide):
        count = count + weight
    sine_x, value_x = sine_table(rows_x + 2)
    sine_y, value_y = sine_table(rows_y + 2)
    sine_z, value_z = sine_table(depth)
    inv_eig = 1.0 / (value_x[:, None, None] + value_y[None, :, None] + value_z[None, None, :])
    inverse = coarse_inverse.astype(jnp.float32)
    count_x = lax.axis_size("gx")
    count_y = lax.axis_size("gy")

    def local_solve(masked, wide=None):
        if wide is None:
            wide = extend(masked)
        spectral = modal(wide, sine_x, sine_y, sine_z) * inv_eig
        return margin_sum(modal(spectral, sine_x, sine_y, sine_z))

    permuted = jnp.transpose(jnp.transpose(inverse[index_map])[index_map])
    me = lax.axis_index(("gx", "gy"))

    def coarse(gathered):
        sol = jnp.dot(permuted, gathered, precision=high)
        return gathered, sol, lax.dynamic_index_in_dim(sol, me, 0, keepdims=False)

    def operate(direction, wide=None):
        if wide is None:
            wide = face_halo(direction)
        padded_field = jnp.pad(wide, ((0, 0), (0, 0), (1, 1)))
        beside = jnp.zeros_like(direction)
        for operate_weight, value in zip(beside_all(fluid_wide), beside_all(padded_field)):
            beside = beside + operate_weight * value
        return fluid * (count * direction - beside) + solid * direction

    inner = fluid_wide[:, :, 1:-1]
    k_row = jnp.stack(
        [
            jnp.sum(fluid * operate(fluid, jnp.pad(fluid, ((1, 1), (1, 1), (0, 0))))),
            -jnp.sum(fluid[0] * inner[0, 1:-1]),
            -jnp.sum(fluid[-1] * inner[-1, 1:-1]),
            -jnp.sum(fluid[:, 0] * inner[1:-1, 0]),
            -jnp.sum(fluid[:, -1] * inner[1:-1, -1]),
        ]
    )

    every = exchange((jnp.sum(masked) / cells).reshape(1), jnp.zeros((0,), jnp.float32))[0]
    vec0, sol0, value0 = coarse(every)
    local0 = local_solve(masked, both_wide[:, :, :depth])
    precond = fluid * (local0 + value0)
    direction = precond

    image = operate(direction)
    masked_w = image * fluid
    local_w = local_solve(masked_w)
    fluid_local_w = fluid * local_w
    image_local_w = operate(fluid_local_w)
    every_w, partial = exchange(
        jnp.concatenate([jnp.stack([jnp.sum(masked_w) / cells, jnp.sum(fluid * image_local_w)]), k_row]),
        jnp.stack(
            [
                jnp.sum(residual * fluid * local0),
                jnp.sum(direction * image),
                jnp.sum(residual * fluid * local_w),
                jnp.sum(image * fluid * local0),
                jnp.sum(image * fluid * local_w),
                jnp.sum(fluid_local_w * image_local_w),
            ]
        ),
    )
    energy_now = partial[0] + cells * jnp.sum(vec0 * sol0)
    partial = partial[1:]
    every_w = every_w.reshape(subdomains, 7)
    k_grid = every_w[:, 2:].reshape(count_x, count_y, 5)
    vec_w, sol_w, value_w = coarse(every_w[:, 0])
    delta_now = partial[0]
    step_size = energy_now / delta_now
    solution = step_size * direction
    residual = residual - step_size * image
    cross_r = partial[1] + cells * jnp.sum(vec0 * sol_w)
    cross_w = partial[2] + cells * jnp.sum(vec_w * sol0)
    square_w = partial[3] + cells * jnp.sum(vec_w * sol_w)
    energy_next = energy_now - step_size * (cross_r + cross_w) + step_size * step_size * square_w
    ratio = energy_next / energy_now
    precond = precond - step_size * (fluid * (local_w + value_w))
    direction = precond + ratio * direction

    coarse_w = sol_w
    grid_w = coarse_w.reshape(count_x, count_y)
    near_w = jnp.stack(
        [
            grid_w,
            jnp.pad(grid_w[:-1], ((1, 0), (0, 0))),
            jnp.pad(grid_w[1:], ((0, 1), (0, 0))),
            jnp.pad(grid_w[:, :-1], ((0, 0), (1, 0))),
            jnp.pad(grid_w[:, 1:], ((0, 0), (0, 1))),
        ],
        axis=-1,
    )
    coarse_energy = jnp.sum(grid_w[:, :, None] * k_grid * near_w)
    square_m = partial[4] + 2.0 * jnp.sum(coarse_w * every_w[:, 1]) + coarse_energy
    grow = 1.0 + ratio
    delta_next = grow * grow * delta_now - 2.0 * step_size * grow * square_w + step_size * step_size * square_m

    mine = near_w[lax.axis_index("gx"), lax.axis_index("gy")]
    coarse_wide = jnp.zeros((rows_x + 2, rows_y + 2, depth), jnp.float32)
    coarse_wide = coarse_wide.at[1:-1, 1:-1].set(fluid * mine[0])
    coarse_wide = coarse_wide.at[0, 1:-1].set(inner[0, 1:-1] * mine[1])
    coarse_wide = coarse_wide.at[-1, 1:-1].set(inner[-1, 1:-1] * mine[2])
    coarse_wide = coarse_wide.at[1:-1, 0].set(inner[1:-1, 0] * mine[3])
    coarse_wide = coarse_wide.at[1:-1, -1].set(inner[1:-1, -1] * mine[4])
    image_m = image_local_w + operate(fluid * mine[0], coarse_wide)
    image = grow * image - step_size * image_m

    step_size = energy_next / delta_next
    solution = solution + step_size * direction
    residual = residual - step_size * image
    return (solution, residual)


def solution(mesh):
    in_specs = (P("gx", "gy", None), P("gx", "gy"), P(), P())
    out_specs = (P("gx", "gy", None), P("gx", "gy", None))
    return jax.shard_map(body, mesh=mesh, in_specs=in_specs, out_specs=out_specs, check_vma=False)
```

```python
import jax
import numpy as np
import jax.numpy as jnp
from jax import lax
from jax.sharding import PartitionSpec as P

ITERS = 2


def with_halo(cells, sides, width):
    for axis, dim in sides:
        count = lax.axis_size(axis)
        ends = count - 1
        head = lax.slice_in_dim(cells, 0, width, axis=dim)
        tail = lax.slice_in_dim(cells, cells.shape[dim] - width, cells.shape[dim], axis=dim)
        cells = jnp.concatenate(
            [
                lax.ppermute(tail, axis, [(i, (i + 1) % count) for i in range(ends)]),
                cells,
                lax.ppermute(head, axis, [((i + 1) % count, i) for i in range(ends)]),
            ],
            axis=dim,
        )
    return cells


def exchange(gathered, summed):
    parts = []
    k1 = gathered.shape[0]
    stage = jnp.concatenate([gathered, summed])
    for axis in ("gy", "gx"):
        count = lax.axis_size(axis)
        got = lax.all_to_all(jnp.broadcast_to(stage[None], (count,) + stage.shape), axis, 0, 0, tiled=False)
        width = got.shape[1] - summed.shape[0]
        summed = jnp.sum(got[:, width:], axis=0)
        gathered = got[:, :width].reshape(-1)
        stage = jnp.concatenate([gathered, summed])
    return gathered, summed


def total(value):
    return exchange(jnp.zeros((0,), jnp.float32), value.reshape(1))[1][0]


def extend(field):
    return with_halo(field, (("gx", 0), ("gy", 1)), 1)


def sine_table(count):
    order = jnp.arange(count, dtype=jnp.float32) + 1.0
    modes = jnp.sqrt(2.0 / (count + 1.0)) * jnp.sin(
        jnp.pi * order[:, None] * order[None, :] / (count + 1.0)
    )
    values = 2.0 - 2.0 * jnp.cos(jnp.pi * order / (count + 1.0))
    return (modes, values)


def beside_all(array):
    return [
        array[2:, 1:-1, 1:-1],
        array[:-2, 1:-1, 1:-1],
        array[1:-1, 2:, 1:-1],
        array[1:-1, :-2, 1:-1],
        array[1:-1, 1:-1, 2:],
        array[1:-1, 1:-1, :-2],
    ]


def modal(block, sine_x, sine_y, sine_z):
    high = lax.Precision.HIGHEST
    section = jnp.einsum("ia,abk->ibk", sine_x, block, precision=high)
    section = jnp.einsum("jb,ibk->ijk", sine_y, section, precision=high)
    return jnp.einsum("kc,ijc->ijk", sine_z, section, precision=high)


def margin_sum(block):
    count_x = lax.axis_size("gx")
    count_y = lax.axis_size("gy")
    up_x = [(i, i + 1) for i in range(count_x - 1)]
    down_x = [(i + 1, i) for i in range(count_x - 1)]
    up_y = [(i, i + 1) for i in range(count_y - 1)]
    down_y = [(i + 1, i) for i in range(count_y - 1)]
    rows_x = block.shape[0] - 2
    rows_y = block.shape[1] - 2
    from_low = lax.ppermute(block[-1:], "gx", up_x)
    from_high = lax.ppermute(block[:1], "gx", down_x)
    body_rows = block[1:-1]
    body_rows = body_rows + jnp.pad(from_low, ((0, rows_x - 1), (0, 0), (0, 0)))
    body_rows = body_rows + jnp.pad(from_high, ((rows_x - 1, 0), (0, 0), (0, 0)))
    from_left = lax.ppermute(body_rows[:, -1:], "gy", up_y)
    from_right = lax.ppermute(body_rows[:, :1], "gy", down_y)
    core = body_rows[:, 1:-1]
    core = core + jnp.pad(from_left, ((0, 0), (0, rows_y - 1), (0, 0)))
    core = core + jnp.pad(from_right, ((0, 0), (rows_y - 1, 0), (0, 0)))
    return core


def overlap_sum(block, extra):
    summed = block
    for axis, dim in (("gx", 0), ("gy", 1)):
        count = lax.axis_size(axis)
        up = [(i, i + 1) for i in range(count - 1)]
        down = [(i + 1, i) for i in range(count - 1)]
        size = summed.shape[dim]
        from_low = lax.ppermute(lax.slice_in_dim(summed, size - extra - 1, size, axis=dim), axis, up)
        from_high = lax.ppermute(lax.slice_in_dim(summed, 0, extra + 1, axis=dim), axis, down)
        if extra == 0:
            own = lax.slice_in_dim(summed, 1, size - 1, axis=dim)
        else:
            widths = [(0, 0)] * summed.ndim
            widths[dim] = (extra - 1, extra - 1)
            own = jnp.pad(summed, widths)
        rows = own.shape[dim]
        widths = [(0, 0)] * summed.ndim
        widths[dim] = (0, rows - extra - 1)
        low = jnp.pad(from_low, widths)
        widths[dim] = (rows - extra - 1, 0)
        summed = own + low + jnp.pad(from_high, widths)
    return summed


def face_halo(cells):
    count_x = lax.axis_size("gx")
    count_y = lax.axis_size("gy")
    up_x = [(i, i + 1) for i in range(count_x - 1)]
    down_x = [(i + 1, i) for i in range(count_x - 1)]
    up_y = [(i, i + 1) for i in range(count_y - 1)]
    down_y = [(i + 1, i) for i in range(count_y - 1)]
    low_x = lax.ppermute(cells[-1:], "gx", up_x)
    high_x = lax.ppermute(cells[:1], "gx", down_x)
    low_y = lax.ppermute(cells[:, -1:], "gy", up_y)
    high_y = lax.ppermute(cells[:, :1], "gy", down_y)
    middle = jnp.concatenate([low_y, cells, high_y], axis=1)
    pad_y = ((0, 0), (1, 1), (0, 0))
    return jnp.concatenate([jnp.pad(low_x, pad_y), middle, jnp.pad(high_x, pad_y)], axis=0)


def body(rhs, heights, index_map, coarse_inverse):
    rows_x, rows_y, depth = rhs.shape
    subdomains = coarse_inverse.shape[0]
    cells = rows_x * rows_y * depth
    high = lax.Precision.HIGHEST
    levels = jnp.arange(depth, dtype=jnp.int32)
    solid = (levels[None, None, :] < heights[:, :, None]).astype(jnp.float32)
    fluid = 1.0 - solid
    residual = fluid * rhs
    masked = residual * fluid
    both_wide = with_halo(jnp.concatenate([masked, solid], axis=2), (("gx", 0), ("gy", 1)), 2)
    solid_two = both_wide[:, :, depth:]
    masked_wide = both_wide[1:-1, 1:-1, :depth]
    solid_side = solid_two[1:-1, 1:-1]
    bottom = jnp.ones((rows_x + 4, rows_y + 4, 1), jnp.float32)
    top = jnp.zeros((rows_x + 4, rows_y + 4, 1), jnp.float32)
    fluid_two = 1.0 - jnp.concatenate([bottom, solid_two, top], 2)
    fluid_wide = fluid_two[1:-1, 1:-1]
    count_wide = jnp.zeros_like(solid_side)
    for weight in beside_all(fluid_two):
        count_wide = count_wide + weight
    count = count_wide[1:-1, 1:-1]
    fluid_one = 1.0 - solid_side
    place_x = lax.axis_index("gx") * rows_x + jnp.arange(rows_x + 4) - 2
    place_y = lax.axis_index("gy") * rows_y + jnp.arange(rows_y + 4) - 2
    inside_x = (place_x >= 0) & (place_x < lax.axis_size("gx") * rows_x)
    inside_y = (place_y >= 0) & (place_y < lax.axis_size("gy") * rows_y)
    inside_two = (inside_x[:, None] & inside_y[None, :]).astype(jnp.float32)[:, :, None]
    inside_one = inside_two[1:-1, 1:-1]
    sine_x, value_x = sine_table(rows_x + 2)
    sine_y, value_y = sine_table(rows_y + 2)
    sine_z, value_z = sine_table(depth)
    inv_eig = 1.0 / (value_x[:, None, None] + value_y[None, :, None] + value_z[None, None, :])
    inverse = coarse_inverse.astype(jnp.float32)
    count_x = lax.axis_size("gx")
    count_y = lax.axis_size("gy")

    def local_solve(wide, extra):
        spectral = modal(wide, sine_x, sine_y, sine_z) * inv_eig
        return overlap_sum(modal(spectral, sine_x, sine_y, sine_z), extra)

    permuted = jnp.transpose(jnp.transpose(inverse[index_map])[index_map])
    me = lax.axis_index(("gx", "gy"))

    def coarse(gathered):
        sol = jnp.dot(permuted, gathered, precision=high)
        return gathered, sol, lax.dynamic_index_in_dim(sol, me, 0, keepdims=False)

    def operate(direction, wide=None):
        if wide is None:
            wide = face_halo(direction)
        padded_field = jnp.pad(wide, ((0, 0), (0, 0), (1, 1)))
        beside = jnp.zeros_like(direction)
        for operate_weight, value in zip(beside_all(fluid_wide), beside_all(padded_field)):
            beside = beside + operate_weight * value
        return fluid * (count * direction - beside) + solid * direction

    inner = fluid_wide[:, :, 1:-1]
    k_row = jnp.stack(
        [
            jnp.sum(fluid * operate(fluid, jnp.pad(fluid, ((1, 1), (1, 1), (0, 0))))),
            -jnp.sum(fluid[0] * inner[0, 1:-1]),
            -jnp.sum(fluid[-1] * inner[-1, 1:-1]),
            -jnp.sum(fluid[:, 0] * inner[1:-1, 0]),
            -jnp.sum(fluid[:, -1] * inner[1:-1, -1]),
        ]
    )

    every = exchange((jnp.sum(masked) / cells).reshape(1), jnp.zeros((0,), jnp.float32))[0]
    vec0, sol0, value0 = coarse(every)
    local0_two = local_solve(masked_wide, 2) * inside_two
    local0 = local0_two[2:-2, 2:-2]
    near0 = lax.dynamic_slice(
        jnp.pad(sol0.reshape(count_x, count_y), 1), (lax.axis_index("gx"), lax.axis_index("gy")), (3, 3)
    )
    spread0 = jnp.repeat(near0, np.array([2, rows_x, 2]), axis=0, total_repeat_length=rows_x + 4)
    spread0 = jnp.repeat(spread0, np.array([2, rows_y, 2]), axis=1, total_repeat_length=rows_y + 4)
    direction_two = (1.0 - solid_two) * (local0_two + spread0[:, :, None])
    direction = direction_two[2:-2, 2:-2]
    precond = direction

    padded_two = jnp.pad(direction_two, ((0, 0), (0, 0), (1, 1)))
    beside = jnp.zeros_like(solid_side)
    for operate_weight, value in zip(beside_all(fluid_two), beside_all(padded_two)):
        beside = beside + operate_weight * value
    centre = direction_two[1:-1, 1:-1]
    image_wide = fluid_one * (count_wide * centre - beside) + solid_side * centre
    image = image_wide[1:-1, 1:-1]
    masked_w_wide = image_wide * fluid_one * inside_one
    masked_w = masked_w_wide[1:-1, 1:-1]
    local_w_wide = local_solve(masked_w_wide, 1) * inside_one
    local_w = local_w_wide[1:-1, 1:-1]
    fluid_local_w = fluid * local_w
    image_local_w = operate(fluid_local_w, fluid_one * local_w_wide)
    every_w, partial = exchange(
        jnp.concatenate([jnp.stack([jnp.sum(masked_w) / cells, jnp.sum(fluid * image_local_w)]), k_row]),
        jnp.stack(
            [
                jnp.sum(residual * fluid * local0),
                jnp.sum(direction * image),
                jnp.sum(residual * fluid * local_w),
                jnp.sum(image * fluid * local0),
                jnp.sum(image * fluid * local_w),
                jnp.sum(fluid_local_w * image_local_w),
            ]
        ),
    )
    energy_now = partial[0] + cells * jnp.sum(vec0 * sol0)
    partial = partial[1:]
    every_w = every_w.reshape(subdomains, 7)
    k_grid = every_w[:, 2:].reshape(count_x, count_y, 5)
    vec_w, sol_w, value_w = coarse(every_w[:, 0])
    delta_now = partial[0]
    step_size = energy_now / delta_now
    solution = step_size * direction
    residual = residual - step_size * image
    cross_r = partial[1] + cells * jnp.sum(vec0 * sol_w)
    cross_w = partial[2] + cells * jnp.sum(vec_w * sol0)
    square_w = partial[3] + cells * jnp.sum(vec_w * sol_w)
    energy_next = energy_now - step_size * (cross_r + cross_w) + step_size * step_size * square_w
    ratio = energy_next / energy_now
    precond = precond - step_size * (fluid * (local_w + value_w))
    direction = precond + ratio * direction

    coarse_w = sol_w
    grid_w = coarse_w.reshape(count_x, count_y)
    near_w = jnp.stack(
        [
            grid_w,
            jnp.pad(grid_w[:-1], ((1, 0), (0, 0))),
            jnp.pad(grid_w[1:], ((0, 1), (0, 0))),
            jnp.pad(grid_w[:, :-1], ((0, 0), (1, 0))),
            jnp.pad(grid_w[:, 1:], ((0, 0), (0, 1))),
        ],
        axis=-1,
    )
    coarse_energy = jnp.sum(grid_w[:, :, None] * k_grid * near_w)
    square_m = partial[4] + 2.0 * jnp.sum(coarse_w * every_w[:, 1]) + coarse_energy
    grow = 1.0 + ratio
    delta_next = grow * grow * delta_now - 2.0 * step_size * grow * square_w + step_size * step_size * square_m

    mine = near_w[lax.axis_index("gx"), lax.axis_index("gy")]
    coarse_wide = jnp.zeros((rows_x + 2, rows_y + 2, depth), jnp.float32)
    coarse_wide = coarse_wide.at[1:-1, 1:-1].set(fluid * mine[0])
    coarse_wide = coarse_wide.at[0, 1:-1].set(inner[0, 1:-1] * mine[1])
    coarse_wide = coarse_wide.at[-1, 1:-1].set(inner[-1, 1:-1] * mine[2])
    coarse_wide = coarse_wide.at[1:-1, 0].set(inner[1:-1, 0] * mine[3])
    coarse_wide = coarse_wide.at[1:-1, -1].set(inner[1:-1, -1] * mine[4])
    image_m = image_local_w + operate(fluid * mine[0], coarse_wide)
    image = grow * image - step_size * image_m

    step_size = energy_next / delta_next
    solution = solution + step_size * direction
    residual = residual - step_size * image
    return (solution, residual)


def solution(mesh):
    in_specs = (P("gx", "gy", None), P("gx", "gy"), P(), P())
    out_specs = (P("gx", "gy", None), P("gx", "gy", None))
    return jax.shard_map(body, mesh=mesh, in_specs=in_specs, out_specs=out_specs, check_vma=False)
```

```python
import jax
import numpy as np
import jax.numpy as jnp
from jax import lax
from jax.sharding import PartitionSpec as P

ITERS = 2


def with_halo(cells, sides, width):
    for axis, dim in sides:
        count = lax.axis_size(axis)
        ends = count - 1
        head = lax.slice_in_dim(cells, 0, width, axis=dim)
        tail = lax.slice_in_dim(cells, cells.shape[dim] - width, cells.shape[dim], axis=dim)
        cells = jnp.concatenate(
            [
                lax.ppermute(tail, axis, [(i, (i + 1) % count) for i in range(ends)]),
                cells,
                lax.ppermute(head, axis, [((i + 1) % count, i) for i in range(ends)]),
            ],
            axis=dim,
        )
    return cells


def exchange(gathered, summed):
    parts = []
    k1 = gathered.shape[0]
    stage = jnp.concatenate([gathered, summed])
    for axis in ("gy", "gx"):
        count = lax.axis_size(axis)
        got = lax.all_to_all(jnp.broadcast_to(stage[None], (count,) + stage.shape), axis, 0, 0, tiled=False)
        width = got.shape[1] - summed.shape[0]
        summed = jnp.sum(got[:, width:], axis=0)
        gathered = got[:, :width].reshape(-1)
        stage = jnp.concatenate([gathered, summed])
    return gathered, summed


def total(value):
    return exchange(jnp.zeros((0,), jnp.float32), value.reshape(1))[1][0]


def extend(field):
    return with_halo(field, (("gx", 0), ("gy", 1)), 1)


def sine_table(count):
    order = jnp.arange(count, dtype=jnp.float32) + 1.0
    modes = jnp.sqrt(2.0 / (count + 1.0)) * jnp.sin(
        jnp.pi * order[:, None] * order[None, :] / (count + 1.0)
    )
    values = 2.0 - 2.0 * jnp.cos(jnp.pi * order / (count + 1.0))
    return (modes, values)


def beside_all(array):
    return [
        array[2:, 1:-1, 1:-1],
        array[:-2, 1:-1, 1:-1],
        array[1:-1, 2:, 1:-1],
        array[1:-1, :-2, 1:-1],
        array[1:-1, 1:-1, 2:],
        array[1:-1, 1:-1, :-2],
    ]


def modal(block, sine_x, sine_y, sine_z):
    high = lax.Precision.HIGHEST
    section = jnp.einsum("ia,abk->ibk", sine_x, block, precision=high)
    section = jnp.einsum("jb,ibk->ijk", sine_y, section, precision=high)
    return jnp.einsum("kc,ijc->ijk", sine_z, section, precision=high)


def margin_sum(block):
    count_x = lax.axis_size("gx")
    count_y = lax.axis_size("gy")
    up_x = [(i, i + 1) for i in range(count_x - 1)]
    down_x = [(i + 1, i) for i in range(count_x - 1)]
    up_y = [(i, i + 1) for i in range(count_y - 1)]
    down_y = [(i + 1, i) for i in range(count_y - 1)]
    rows_x = block.shape[0] - 2
    rows_y = block.shape[1] - 2
    from_low = lax.ppermute(block[-1:], "gx", up_x)
    from_high = lax.ppermute(block[:1], "gx", down_x)
    body_rows = block[1:-1]
    body_rows = body_rows + jnp.pad(from_low, ((0, rows_x - 1), (0, 0), (0, 0)))
    body_rows = body_rows + jnp.pad(from_high, ((rows_x - 1, 0), (0, 0), (0, 0)))
    from_left = lax.ppermute(body_rows[:, -1:], "gy", up_y)
    from_right = lax.ppermute(body_rows[:, :1], "gy", down_y)
    core = body_rows[:, 1:-1]
    core = core + jnp.pad(from_left, ((0, 0), (0, rows_y - 1), (0, 0)))
    core = core + jnp.pad(from_right, ((0, 0), (rows_y - 1, 0), (0, 0)))
    return core


def overlap_sum(block, extra):
    summed = block
    for axis, dim in (("gx", 0), ("gy", 1)):
        count = lax.axis_size(axis)
        up = [(i, i + 1) for i in range(count - 1)]
        down = [(i + 1, i) for i in range(count - 1)]
        size = summed.shape[dim]
        from_low = lax.ppermute(lax.slice_in_dim(summed, size - extra - 1, size, axis=dim), axis, up)
        from_high = lax.ppermute(lax.slice_in_dim(summed, 0, extra + 1, axis=dim), axis, down)
        if extra == 0:
            own = lax.slice_in_dim(summed, 1, size - 1, axis=dim)
        else:
            widths = [(0, 0)] * summed.ndim
            widths[dim] = (extra - 1, extra - 1)
            own = jnp.pad(summed, widths)
        rows = own.shape[dim]
        widths = [(0, 0)] * summed.ndim
        widths[dim] = (0, rows - extra - 1)
        low = jnp.pad(from_low, widths)
        widths[dim] = (rows - extra - 1, 0)
        summed = own + low + jnp.pad(from_high, widths)
    return summed


def face_halo(cells):
    count_x = lax.axis_size("gx")
    count_y = lax.axis_size("gy")
    up_x = [(i, i + 1) for i in range(count_x - 1)]
    down_x = [(i + 1, i) for i in range(count_x - 1)]
    up_y = [(i, i + 1) for i in range(count_y - 1)]
    down_y = [(i + 1, i) for i in range(count_y - 1)]
    low_x = lax.ppermute(cells[-1:], "gx", up_x)
    high_x = lax.ppermute(cells[:1], "gx", down_x)
    low_y = lax.ppermute(cells[:, -1:], "gy", up_y)
    high_y = lax.ppermute(cells[:, :1], "gy", down_y)
    middle = jnp.concatenate([low_y, cells, high_y], axis=1)
    pad_y = ((0, 0), (1, 1), (0, 0))
    return jnp.concatenate([jnp.pad(low_x, pad_y), middle, jnp.pad(high_x, pad_y)], axis=0)


def body(rhs, heights, index_map, coarse_inverse):
    rows_x, rows_y, depth = rhs.shape
    subdomains = coarse_inverse.shape[0]
    cells = rows_x * rows_y * depth
    high = lax.Precision.HIGHEST
    levels = jnp.arange(depth, dtype=jnp.int32)
    solid = (levels[None, None, :] < heights[:, :, None]).astype(jnp.float32)
    fluid = 1.0 - solid
    residual = fluid * rhs
    masked = residual * fluid
    both_wide = with_halo(jnp.concatenate([masked, solid], axis=2), (("gx", 0), ("gy", 1)), 2)
    solid_two = both_wide[:, :, depth:]
    masked_wide = both_wide[1:-1, 1:-1, :depth]
    solid_side = solid_two[1:-1, 1:-1]
    bottom = jnp.ones((rows_x + 4, rows_y + 4, 1), jnp.float32)
    top = jnp.zeros((rows_x + 4, rows_y + 4, 1), jnp.float32)
    fluid_two = 1.0 - jnp.concatenate([bottom, solid_two, top], 2)
    fluid_wide = fluid_two[1:-1, 1:-1]
    count_wide = jnp.zeros_like(solid_side)
    for weight in beside_all(fluid_two):
        count_wide = count_wide + weight
    count = count_wide[1:-1, 1:-1]
    fluid_one = 1.0 - solid_side
    place_x = lax.axis_index("gx") * rows_x + jnp.arange(rows_x + 4) - 2
    place_y = lax.axis_index("gy") * rows_y + jnp.arange(rows_y + 4) - 2
    inside_x = (place_x >= 0) & (place_x < lax.axis_size("gx") * rows_x)
    inside_y = (place_y >= 0) & (place_y < lax.axis_size("gy") * rows_y)
    inside_two = (inside_x[:, None] & inside_y[None, :]).astype(jnp.float32)[:, :, None]
    inside_one = inside_two[1:-1, 1:-1]
    sine_x, value_x = sine_table(rows_x + 2)
    sine_y, value_y = sine_table(rows_y + 2)
    sine_z, value_z = sine_table(depth)
    inv_eig = 1.0 / (value_x[:, None, None] + value_y[None, :, None] + value_z[None, None, :])
    inverse = coarse_inverse.astype(jnp.float32)
    count_x = lax.axis_size("gx")
    count_y = lax.axis_size("gy")

    def local_solve(wide, extra):
        spectral = modal(wide, sine_x, sine_y, sine_z) * inv_eig
        return overlap_sum(modal(spectral, sine_x, sine_y, sine_z), extra)

    permuted = jnp.transpose(jnp.transpose(inverse[index_map])[index_map])
    me = lax.axis_index(("gx", "gy"))

    def coarse(gathered):
        sol = jnp.dot(permuted, gathered, precision=high)
        return gathered, sol, lax.dynamic_index_in_dim(sol, me, 0, keepdims=False)

    def operate(direction, wide=None):
        if wide is None:
            wide = face_halo(direction)
        padded_field = jnp.pad(wide, ((0, 0), (0, 0), (1, 1)))
        beside = jnp.zeros_like(direction)
        for operate_weight, value in zip(beside_all(fluid_wide), beside_all(padded_field)):
            beside = beside + operate_weight * value
        return fluid * (count * direction - beside) + solid * direction

    inner = fluid_wide[:, :, 1:-1]
    basis = [
        operate(fluid, jnp.pad(fluid, ((1, 1), (1, 1), (0, 0)))),
        jnp.pad(-(fluid[:1] * inner[:1, 1:-1]), ((0, rows_x - 1), (0, 0), (0, 0))),
        jnp.pad(-(fluid[-1:] * inner[-1:, 1:-1]), ((rows_x - 1, 0), (0, 0), (0, 0))),
        jnp.pad(-(fluid[:, :1] * inner[1:-1, :1]), ((0, 0), (0, rows_y - 1), (0, 0))),
        jnp.pad(-(fluid[:, -1:] * inner[1:-1, -1:]), ((0, 0), (rows_y - 1, 0), (0, 0))),
    ]
    k_row = jnp.stack(
        [
            jnp.sum(fluid * basis[0]),
            -jnp.sum(fluid[0] * inner[0, 1:-1]),
            -jnp.sum(fluid[-1] * inner[-1, 1:-1]),
            -jnp.sum(fluid[:, 0] * inner[1:-1, 0]),
            -jnp.sum(fluid[:, -1] * inner[1:-1, -1]),
        ]
    )

    every = exchange((jnp.sum(masked) / cells).reshape(1), jnp.zeros((0,), jnp.float32))[0]
    vec0, sol0, value0 = coarse(every)
    local0_two = local_solve(masked_wide, 2) * inside_two
    local0 = local0_two[2:-2, 2:-2]
    near0 = lax.dynamic_slice(
        jnp.pad(sol0.reshape(count_x, count_y), 1), (lax.axis_index("gx"), lax.axis_index("gy")), (3, 3)
    )
    spread0 = jnp.repeat(near0, np.array([2, rows_x, 2]), axis=0, total_repeat_length=rows_x + 4)
    spread0 = jnp.repeat(spread0, np.array([2, rows_y, 2]), axis=1, total_repeat_length=rows_y + 4)
    direction_two = (1.0 - solid_two) * (local0_two + spread0[:, :, None])
    direction = direction_two[2:-2, 2:-2]
    precond = direction

    padded_two = jnp.pad(direction_two, ((0, 0), (0, 0), (1, 1)))
    beside = jnp.zeros_like(solid_side)
    for operate_weight, value in zip(beside_all(fluid_two), beside_all(padded_two)):
        beside = beside + operate_weight * value
    centre = direction_two[1:-1, 1:-1]
    image_wide = fluid_one * (count_wide * centre - beside) + solid_side * centre
    image = image_wide[1:-1, 1:-1]
    masked_w_wide = image_wide * fluid_one * inside_one
    masked_w = masked_w_wide[1:-1, 1:-1]
    local_w_wide = local_solve(masked_w_wide, 1) * inside_one
    local_w = local_w_wide[1:-1, 1:-1]
    fluid_local_w = fluid * local_w
    image_local_w = operate(fluid_local_w, fluid_one * local_w_wide)
    every_w, partial = exchange(
        jnp.concatenate([jnp.stack([jnp.sum(masked_w) / cells, jnp.sum(fluid * image_local_w)]), k_row]),
        jnp.stack(
            [
                jnp.sum(residual * fluid * local0),
                jnp.sum(direction * image),
                jnp.sum(residual * fluid * local_w),
                jnp.sum(image * fluid * local0),
                jnp.sum(image * fluid * local_w),
                jnp.sum(fluid_local_w * image_local_w),
            ]
        ),
    )
    energy_now = partial[0] + cells * jnp.sum(vec0 * sol0)
    partial = partial[1:]
    every_w = every_w.reshape(subdomains, 7)
    k_grid = every_w[:, 2:].reshape(count_x, count_y, 5)
    vec_w, sol_w, value_w = coarse(every_w[:, 0])
    delta_now = partial[0]
    step_size = energy_now / delta_now
    cross_r = partial[1] + cells * jnp.sum(vec0 * sol_w)
    cross_w = partial[2] + cells * jnp.sum(vec_w * sol0)
    square_w = partial[3] + cells * jnp.sum(vec_w * sol_w)
    energy_next = energy_now - step_size * (cross_r + cross_w) + step_size * step_size * square_w
    ratio = energy_next / energy_now

    coarse_w = sol_w
    grid_w = coarse_w.reshape(count_x, count_y)
    near_w = jnp.stack(
        [
            grid_w,
            jnp.pad(grid_w[:-1], ((1, 0), (0, 0))),
            jnp.pad(grid_w[1:], ((0, 1), (0, 0))),
            jnp.pad(grid_w[:, :-1], ((0, 0), (1, 0))),
            jnp.pad(grid_w[:, 1:], ((0, 0), (0, 1))),
        ],
        axis=-1,
    )
    coarse_energy = jnp.sum(grid_w[:, :, None] * k_grid * near_w)
    square_m = partial[4] + 2.0 * jnp.sum(coarse_w * every_w[:, 1]) + coarse_energy
    grow = 1.0 + ratio
    delta_next = grow * grow * delta_now - 2.0 * step_size * grow * square_w + step_size * step_size * square_m
    last_step = energy_next / delta_next

    mine = near_w[lax.axis_index("gx"), lax.axis_index("gy")]
    lead = step_size + last_step * grow
    both = last_step * step_size
    coarse_image = (
        mine[0] * basis[0] + mine[1] * basis[1] + mine[2] * basis[2] + mine[3] * basis[3] + mine[4] * basis[4]
    )
    solution = lead * direction - both * (fluid_local_w + fluid * value_w)
    residual = residual - lead * image + both * (image_local_w + coarse_image)
    return (solution, residual)


def solution(mesh):
    in_specs = (P("gx", "gy", None), P("gx", "gy"), P(), P())
    out_specs = (P("gx", "gy", None), P("gx", "gy", None))
    return jax.shard_map(body, mesh=mesh, in_specs=in_specs, out_specs=out_specs, check_vma=False)
```
